32 devices in a mesh: expert: 4 (over z), dp: 8 (over y, x, core).
Axes of the slice: x: 2, y: 2, z: 4, core: 2. Of those that a mesh axis runs over, the one named last changes fastest.
Arguments:
- tokens: bfloat16 [4096, 3584], P(('expert', 'dp')), may hold values from -6 to 6
- cotangent: bfloat16 [4096, 3584], P(('expert', 'dp')), may hold values from -1.5 to 1.5
- block_expert: int32 [256, 1], P(('expert', 'dp')), may hold values from 0 to 3; in each aligned block of 8 rows (0 to 7, 8 to 15, ...) at most 4 rows name the same one
- block_count: int32 [256], P(('expert', 'dp')), may hold values from 8 to 16
- old_owner: int32 [4], replicated, may hold values from 0 to 3, as said below
- new_owner: int32 [4], replicated, may hold values from 0 to 3, as said below
- up_weight: float32 [4, 3584, 1024], P('expert', 'dp'), may hold values from -0.09375 to 0.09375
- down_weight: float32 [4, 1024, 3584], P('expert', 'dp'), may hold values from -0.1875 to 0.1875
- up_first: float32 [4, 3584, 1024], P('expert', 'dp'), may hold values from -6 to 6
- up_second: float32 [4, 3584, 1024], P('expert', 'dp'), may hold values from 1 to 100
- down_first: float32 [4, 1024, 3584], P('expert', 'dp'), may hold values from -6 to 6
- down_second: float32 [4, 1024, 3584], P('expert', 'dp'), may hold values from 1 to 100
Outputs:
- token_grad: bfloat16 [4096, 3584], P(('expert', 'dp'))
- up_weight_new: float32 [4, 3584, 1024], P('expert', 'dp')
- down_weight_new: float32 [4, 1024, 3584], P('expert', 'dp')
- up_first_new: float32 [4, 3584, 1024], P('expert', 'dp')
- up_second_new: float32 [4, 3584, 1024], P('expert', 'dp')
- down_first_new: float32 [4, 1024, 3584], P('expert', 'dp')
- down_second_new: float32 [4, 1024, 3584], P('expert', 'dp')
The draws below stay inside these ranges and needn't reach their ends.
Inputs may be any that keep to these rules, and one draw needn't show every extreme that they name: `block_expert`: among the 8 blocks of one device, at most 4 are routed to any one expert, and in every draw some device routes exactly 4 blocks to some expert. A permutation: each slot appears once, and expert k is held by slot old_owner[k] before the step. A permutation: each slot appears once, and expert k is held by slot new_owner[k] after the step.
All inputs are finite; a program needn't handle non-finite values.
Results may differ from the reference program's by a relative error of at most 0.019.
Values may be sent and summed in bfloat16 or wider, within the bound.
A program may use at most 192 MiB of HBM per device.

```python
import math
import jax
import jax.numpy as jnp
import numpy as np
from jax import lax

D = 3584
FF = 1024
BLOCK_TOK = 16
BLOCKS_DEV = 8
CAPACITY = 4
EXPERTS = 4
TOKENS = 4096
BLOCKS = 256
N_EXPERT = 4
N_DP = 8


def ranked_order(key, salt):
    inner = jax.random.fold_in(key, salt)
    scores = jax.random.randint(inner, (EXPERTS,), 0, 1 << 20, dtype=jnp.int32)
    distinct = scores * EXPERTS + jnp.arange(EXPERTS, dtype=jnp.int32)
    return jnp.argsort(distinct, stable=True).astype(jnp.int32)


def draw_old_owner(key, part):
    return ranked_order(key, 7101)


def draw_new_owner(key, part):
    return ranked_order(key, 9203)


def place_ends(drawn, own_key, smallest, top_value):
    longest = drawn.shape.index(max(drawn.shape))
    spots = []
    for shift in (0, 1):
        where = [jax.random.randint(jax.random.fold_in(own_key, axis), (), 0, length) for axis, length in enumerate(drawn.shape)]
        where[longest] = (where[longest] + shift) % drawn.shape[longest]
        spots.append(tuple(where))
    return drawn.at[spots[0]].set(smallest).at[spots[1]].set(top_value)


def with_spikes(drawn, stream_key, source, target, blocks, factor):
    owner, partner = [(jnp.arange(drawn.shape[axis_at]) // (drawn.shape[axis_at] // blocks)).reshape([-1 if axis == axis_at else 1 for axis in range(drawn.ndim)]) for axis_at in (source, target)]
    chosen = jax.random.permutation(stream_key, blocks)[partner]
    strong = (owner == chosen) | (owner == (partner + blocks // 2) % blocks)
    return jnp.where(strong, factor * drawn, drawn)


def block_scale(stream_key, extent, pieces, least, high):
    def one(dim, shards_of):
        heights = jax.random.uniform(jax.random.fold_in(jax.random.fold_in(stream_key, 6), dim), (shards_of,), jnp.float32, least / len(pieces), high / len(pieces))
        return jnp.repeat(jnp.exp(heights), extent[dim] // shards_of).reshape((-1,) + (1,) * (len(extent) - dim - 1))

    gain = one(*pieces[0])
    for cut in pieces[1:]:
        gain = gain * one(*cut)
    return gain


def assign_block(rng, own, number, rows, count, top, bound, slope):
    ranking = jax.random.permutation(rng, count)
    heavy_load, common = portions_of(count, rows * top, bound, slope, True), portions_of(count, rows * top, bound, slope, False)
    places = jnp.arange(count)

    def named(lengths, offset_by):
        used = int((lengths > 0).sum())
        fixed = max(1, used // 4)
        passed = fixed + (places - fixed + offset_by * (used - fixed)) % max(1, count - fixed)
        return jnp.zeros((count,), jnp.int32).at[ranking[jnp.where(places < fixed, places, passed)]].set(jnp.asarray(lengths, jnp.int32))

    lengths = jnp.where(number % 4 == 0, named(heavy_load, number // 4), named(common, number - number // 4 - 1))
    mixed = jax.random.permutation(jax.random.fold_in(own, 3), count)
    donor, taker = mixed[0:count // 2 * 2:2], mixed[1:count // 2 * 2:2]
    room = jnp.minimum(lengths[donor] - 1, bound - lengths[taker]) // 2
    room = jnp.where((donor == ranking[0]) | (taker == ranking[0]) | (lengths[taker] == 0), 0, jnp.maximum(room, 0))
    passed = jax.random.randint(jax.random.fold_in(own, 4), (count // 2,), 0, 1 << 20) % (room + 1)
    lengths = lengths.at[donor].add(-passed).at[taker].add(passed)
    items = jnp.searchsorted(jnp.cumsum(lengths), jnp.arange(rows * top), side="right").astype(jnp.int32)
    table = items.reshape(top, rows).T
    table = table[jax.random.permutation(jax.random.fold_in(own, 1), rows)]
    offset_by = jax.random.randint(jax.random.fold_in(own, 2), (rows, 1), 0, top)
    return jnp.take_along_axis(table, (jnp.arange(top)[None, :] + offset_by) % top, axis=1)


def portions_of(count, total, most, skew, full):
    loads = [(1 << 20) // math.isqrt(rank ** skew) + 1 for rank in range(1, count + 1)]
    largest = most if full else min(most, max(-(-total // count), total * loads[0] // sum(loads)))
    least = 1 if total - largest >= count - 1 else 0
    given, surplus = [largest] + [least] * (count - 1), total - largest - least * (count - 1)
    while surplus > 0:
        candidates = [i for i in range(1, count) if given[i] < largest] or [i for i in range(1, count) if given[i] < most]
        mass, remaining = sum([loads[i] for i in candidates]), surplus
        for i in candidates:
            extra = min(most - given[i], max(1, remaining * loads[i] // mass), surplus)
            given[i] = given[i] + extra
            surplus = surplus - extra
    return np.array(given)


def bell_draw(key, extent, spread, most, cuts=(), held_as=jnp.bfloat16):
    gain = block_scale(key, extent, cuts, -0.22, 0.18) if cuts else 1.0
    result = jax.random.normal(key, extent, jnp.float32) * spread * gain
    return jnp.minimum(jnp.maximum(result, -most), most).astype(held_as)


def heavy_noise(own_key, shape, deviation, reach, pieces, heavy, kind=jnp.bfloat16):
    array = deviation * jax.random.normal(own_key, shape, jnp.float32)
    if pieces:
        array = array * block_scale(own_key, shape, pieces, -0.22, 0.18)
    return jnp.clip(with_spikes(array, jax.random.fold_in(own_key, 3), *heavy), -reach, reach).astype(kind)


def setup_inputs(seed: int = 0) -> dict:
    splits = jax.random.split(jax.random.key(seed), 13)
    tokens = heavy_noise(splits[0], (TOKENS, D), 1.0, 6.0, ((0, 32),), (0, 1, 32, 2.75))
    cotangent = bell_draw(splits[1], (TOKENS, D), 0.25, 1.5, ((0, 32),))
    block_expert_keys = jax.random.split(jax.random.fold_in(splits[2], 1), BLOCKS // BLOCKS_DEV)
    block_expert_turns = jax.random.permutation(jax.random.fold_in(splits[2], 3), BLOCKS // BLOCKS_DEV)
    block_expert = jax.vmap(lambda own, number: assign_block(jax.random.fold_in(splits[2], 2), own, number, BLOCKS_DEV, EXPERTS, 1, CAPACITY, 2))(block_expert_keys, block_expert_turns).reshape((BLOCKS, 1))
    block_count = place_ends(jax.random.randint(splits[3], (BLOCKS,), BLOCK_TOK // 2, BLOCK_TOK + 1), jax.random.fold_in(splits[3], 1), BLOCK_TOK // 2, BLOCK_TOK).astype(jnp.int32)
    old_owner = draw_old_owner(jax.random.fold_in(splits[12], 71), 0)
    new_owner = draw_new_owner(jax.random.fold_in(splits[12], 71), 0)
    up_weight = bell_draw(splits[6], (EXPERTS, D, FF), D ** -0.5, 0.09375, ((0, 4), (1, 8)), jnp.float32)
    down_weight = bell_draw(splits[7], (EXPERTS, FF, D), FF ** -0.5, 0.1875, ((0, 4), (1, 8)), jnp.float32)
    up_first = bell_draw(splits[8], (EXPERTS, D, FF), 1.0, 6.0, ((0, 4), (1, 8)), jnp.float32)
    up_second = jnp.clip(jnp.exp(math.log(100.0) - 4.6051702 * jax.random.uniform(splits[9], (EXPERTS, D, FF), jnp.float32) ** block_scale(splits[9], (EXPERTS, D, FF), ((0, 4), (1, 8)), -0.2, 0.2)), 1.0, 100.0)
    down_first = bell_draw(splits[10], (EXPERTS, FF, D), 1.0, 6.0, ((0, 4), (1, 8)), jnp.float32)
    down_second = jnp.clip(jnp.exp(math.log(100.0) - 4.6051702 * jax.random.uniform(splits[11], (EXPERTS, FF, D), jnp.float32) ** block_scale(splits[11], (EXPERTS, FF, D), ((0, 4), (1, 8)), -0.2, 0.2)), 1.0, 100.0)
    return dict(tokens=tokens, cotangent=cotangent, block_expert=block_expert, block_count=block_count, old_owner=old_owner, new_owner=new_owner, up_weight=up_weight, down_weight=down_weight, up_first=up_first, up_second=up_second, down_first=down_first, down_second=down_second)


beta_one = 0.9
beta_two = 0.95
bias_one = 1.0 - 0.9 ** 10
bias_two = 1.0 - 0.95 ** 10
rate_value = 0.01
decay_value = 0.1
eps_value = 1e-08

def silu_parts(pre_act):
    sigma = jax.nn.sigmoid(pre_act)
    return (pre_act * sigma, sigma * (1.0 + pre_act * (1.0 - sigma)))

def adam_update(weight, moment, second, gradient):
    moment_new = beta_one * moment + (1.0 - beta_one) * gradient
    second_new = beta_two * second + (1.0 - beta_two) * gradient * gradient
    update = moment_new / bias_one / (jnp.sqrt(second_new / bias_two) + eps_value)
    return (weight - rate_value * (update + decay_value * weight), moment_new, second_new)

def reference(tokens, cotangent, block_expert, block_count, old_owner, new_owner, up_weight, down_weight, up_first, up_second, down_first, down_second):
    groups = N_EXPERT
    ranks = N_DP
    shape = (groups, ranks, BLOCKS_DEV, BLOCK_TOK, D)
    counts = block_count.reshape(groups, ranks, BLOCKS_DEV)
    alive = jnp.arange(BLOCK_TOK, dtype=jnp.int32)[None, None, None, :] < counts[..., None]
    inputs = jnp.where(alive[..., None], tokens.reshape(shape), jnp.zeros((), tokens.dtype))
    upstream = jnp.where(alive[..., None], cotangent.reshape(shape), jnp.zeros((), cotangent.dtype))
    block_ids = block_expert.reshape(groups, ranks, BLOCKS_DEV)
    earlier = jnp.arange(BLOCKS_DEV, dtype=jnp.int32)[:, None] > jnp.arange(BLOCKS_DEV, dtype=jnp.int32)[None, :]
    same_id = block_ids[..., :, None] == block_ids[..., None, :]
    position = lax.optimization_barrier(jnp.sum(same_id & earlier, axis=-1)).astype(jnp.int32)
    up_expert = up_weight[old_owner].astype(jnp.bfloat16)
    down_expert = down_weight[old_owner].astype(jnp.bfloat16)
    slots = jnp.arange(CAPACITY, dtype=jnp.int32)

    def one_rank(totals, members):
        rank_x, rank_dy, rank_ids, rank_pos = members
        rank_xf = rank_x.astype(jnp.float32)
        rank_dyf = rank_dy.astype(jnp.float32)

        def one_expert(gathered, expert):
            pick = ((rank_ids == expert)[:, None, :] & (rank_pos[:, None, :] == slots[None, :, None])).astype(jnp.float32)
            rows_x = jnp.einsum('erb,ebtd->ertd', pick, rank_xf).reshape(-1, D).astype(jnp.bfloat16)
            rows_dy = jnp.einsum('erb,ebtd->ertd', pick, rank_dyf).reshape(-1, D).astype(jnp.bfloat16)
            up_mat = up_expert[expert]
            down_mat = down_expert[expert]
            pre_act = jnp.dot(rows_x, up_mat, preferred_element_type=jnp.float32)
            active, slopes = silu_parts(pre_act)
            hidden = active.astype(jnp.bfloat16)
            back_grad = jnp.dot(rows_dy, down_mat.T, preferred_element_type=jnp.float32)
            pre_grad = (back_grad * slopes).astype(jnp.bfloat16)
            rows_grad = jnp.dot(pre_grad, up_mat.T, preferred_element_type=jnp.float32).astype(jnp.bfloat16)
            up_part = jnp.dot(rows_x.T, pre_grad, preferred_element_type=jnp.float32).astype(jnp.bfloat16)
            down_part = jnp.dot(hidden.T, rows_dy, preferred_element_type=jnp.float32).astype(jnp.bfloat16)
            placed = jnp.einsum('erb,ertd->ebtd', pick, rows_grad.reshape(groups, CAPACITY, BLOCK_TOK, D).astype(jnp.float32))
            return (gathered + placed, (up_part, down_part))
        start = jnp.zeros((groups, BLOCKS_DEV, BLOCK_TOK, D), jnp.float32)
        grads_here, parts = lax.scan(one_expert, start, jnp.arange(EXPERTS, dtype=jnp.int32))
        new_totals = (totals[0] + parts[0].astype(jnp.float32), totals[1] + parts[1].astype(jnp.float32))
        return (new_totals, grads_here.astype(jnp.bfloat16))
    init = (jnp.zeros((EXPERTS, D, FF), jnp.float32), jnp.zeros((EXPERTS, FF, D), jnp.float32))
    members = (inputs.transpose(1, 0, 2, 3, 4), upstream.transpose(1, 0, 2, 3, 4), block_ids.transpose(1, 0, 2), position.transpose(1, 0, 2))
    totals, grads_all = lax.scan(one_rank, init, members)
    token_grad = grads_all.transpose(1, 0, 2, 3, 4).reshape(TOKENS, D)
    up_new = adam_update(up_weight[old_owner], up_first[old_owner], up_second[old_owner], totals[0])
    down_new = adam_update(down_weight[old_owner], down_first[old_owner], down_second[old_owner], totals[1])
    incoming = jnp.zeros((EXPERTS,), jnp.int32).at[new_owner].set(jnp.arange(EXPERTS, dtype=jnp.int32))
    return (token_grad, up_new[0][incoming], down_new[0][incoming], up_new[1][incoming], up_new[2][incoming], down_new[1][incoming], down_new[2][incoming])
```

```python
import itertools

import jax
import jax.numpy as jnp
import numpy as np
from jax import lax
from jax.sharding import PartitionSpec as P

beta_one = 0.9
beta_two = 0.95
bias_one = 1.0 - 0.9**10
bias_two = 1.0 - 0.95**10
rate_value = 0.01
decay_value = 0.1
eps_value = 1e-08


def silu_parts(pre_act):
    sigma = jax.nn.sigmoid(pre_act)
    return (pre_act * sigma, sigma * (1.0 + pre_act * (1.0 - sigma)))


def adam_update(weight, moment, second, gradient):
    moment_new = beta_one * moment + (1.0 - beta_one) * gradient
    second_new = beta_two * second + (1.0 - beta_two) * gradient * gradient
    update = moment_new / bias_one / (jnp.sqrt(second_new / bias_two) + eps_value)
    return (weight - rate_value * (update + decay_value * weight), moment_new, second_new)


def contract_rows(left, right):
    return lax.dot_general(
        left, right, (((0,), (0,)), ((), ())), preferred_element_type=jnp.float32
    )


def slot_permutation(old_owner, new_owner, groups):
    labels = jnp.arange(groups, dtype=jnp.int32)
    dest = jnp.sum(jnp.where(old_owner[:, None] == labels[None, :], new_owner[:, None], 0), axis=0)
    source = jnp.sum(jnp.where(new_owner[:, None] == labels[None, :], old_owner[:, None], 0), axis=0)
    return dest, source


def make_mover(old_owner, new_owner, groups):
    dest, source = slot_permutation(old_owner, new_owner, groups)
    if groups <= 4:
        orders = list(itertools.permutations(range(groups)))
        table = jnp.asarray(np.array(orders, np.int32))
        match = jnp.all(table == dest[None, :], axis=1)
        number = jnp.sum(jnp.where(match, jnp.arange(len(orders), dtype=jnp.int32), 0))

        def branch(order):
            pairs = [(s, d) for s, d in enumerate(order)]
            if all(s == d for s, d in pairs):
                return lambda arrays: arrays
            return lambda arrays: tuple(lax.ppermute(a, "expert", pairs) for a in arrays)

        branches = [branch(order) for order in orders]
        return lambda arrays: lax.switch(number, branches, arrays)

    mine = source[lax.axis_index("expert")]

    def gather_move(arrays):
        return tuple(
            lax.dynamic_index_in_dim(
                lax.all_gather(a, "expert", axis=0, tiled=False), mine, 0, keepdims=False
            )
            for a in arrays
        )

    return gather_move


def local(
    tokens,
    cotangent,
    block_expert,
    block_count,
    old_owner,
    new_owner,
    up_weight,
    down_weight,
    up_first,
    up_second,
    down_first,
    down_second,
):
    groups = lax.axis_size("expert")
    tok_rows, features = tokens.shape
    block_num = block_count.shape[0]
    block_len = tok_rows // block_num
    capacity = 2 * block_num // groups
    move = make_mover(old_owner, new_owner, groups)

    def short(array):
        return array[0].astype(jnp.bfloat16)

    labels = jnp.arange(groups, dtype=jnp.int32)
    block_ids = block_expert[:, 0]
    target = jnp.sum(
        jnp.where(block_ids[:, None] == labels[None, :], new_owner[None, :], 0), axis=1
    )
    earlier = (
        jnp.arange(block_num, dtype=jnp.int32)[:, None]
        > jnp.arange(block_num, dtype=jnp.int32)[None, :]
    )
    same_id = block_ids[:, None] == block_ids[None, :]
    position = jnp.sum(same_id & earlier, axis=1)
    slot_of = target * capacity + position
    placing = (jnp.arange(groups * capacity, dtype=jnp.int32)[:, None] == slot_of[None, :]).astype(
        jnp.bfloat16
    )
    alive = jnp.arange(block_len, dtype=jnp.int32)[None, :] < block_count[:, None]
    zero_value = jnp.zeros((), jnp.bfloat16)

    def dispatch(array):
        blocks = jnp.where(
            alive[:, :, None], array.reshape(block_num, block_len, features), zero_value
        )
        placed = jnp.einsum(
            "sb,btf->stf", placing, blocks, preferred_element_type=jnp.float32
        ).astype(jnp.bfloat16)
        return placed.reshape(groups, capacity * block_len, features)

    def swap(array):
        return lax.all_to_all(array, "expert", split_axis=0, concat_axis=0, tiled=True)

    send_x = dispatch(tokens)
    send_dy = dispatch(cotangent)
    rows = groups * capacity * block_len

    (up_state,) = move((short(up_weight),))
    up_mat = lax.all_gather(up_state, "dp", axis=0, tiled=True)
    down_in, up_state = lax.optimization_barrier((short(down_weight), up_state))
    (down_state,) = move((down_in,))
    down_mat = lax.all_gather(down_state, "dp", axis=0, tiled=True)

    send_x, send_dy, down_state = lax.optimization_barrier((send_x, send_dy, down_state))
    inputs = swap(send_x).reshape(rows, features)
    upstream = swap(send_dy).reshape(rows, features)

    pre_act = jnp.dot(inputs, up_mat, preferred_element_type=jnp.float32)
    active, slopes = silu_parts(pre_act)
    hidden = active.astype(jnp.bfloat16)
    down_part = contract_rows(hidden, upstream).astype(jnp.bfloat16)
    down_grad = lax.psum_scatter(down_part, "dp", scatter_dimension=0, tiled=True)
    back_grad = lax.dot_general(
        upstream, down_mat, (((1,), (1,)), ((), ())), preferred_element_type=jnp.float32
    )
    pre_grad = (back_grad * slopes).astype(jnp.bfloat16)
    up_part = contract_rows(inputs, pre_grad).astype(jnp.bfloat16)
    up_grad = lax.psum_scatter(up_part, "dp", scatter_dimension=0, tiled=True)
    input_grad = lax.dot_general(
        pre_grad, up_mat, (((1,), (1,)), ((), ())), preferred_element_type=jnp.float32
    ).astype(jnp.bfloat16)

    moments = (short(down_first), short(down_second), short(up_first), short(up_second))
    moments, input_grad, _ = lax.optimization_barrier((moments, input_grad, up_part))
    returned = swap(input_grad.reshape(groups, capacity * block_len, features))
    moments, returned = lax.optimization_barrier((moments, returned))
    down_moment, down_square, up_moment, up_square = move(moments)
    token_grad = jnp.einsum(
        "sb,stf->btf",
        placing,
        returned.reshape(groups * capacity, block_len, features),
        preferred_element_type=jnp.float32,
    )
    token_grad = token_grad.astype(jnp.bfloat16).reshape(tok_rows, features)

    def wide(*arrays):
        return tuple(a.astype(jnp.float32) for a in arrays)

    up_new = adam_update(*wide(up_state, up_moment, up_square, up_grad))
    down_new = adam_update(*wide(down_state, down_moment, down_square, down_grad))
    results = (up_new[0], down_new[0], up_new[1], up_new[2], down_new[1], down_new[2])
    return (token_grad,) + tuple(r[None] for r in results)


def solution(mesh):
    state = P("expert", "dp", None)
    row = P(("expert", "dp"), None)
    return jax.shard_map(
        local,
        mesh=mesh,
        in_specs=(row, row, row, P(("expert", "dp")), P(), P()) + (state,) * 6,
        out_specs=(row,) + (state,) * 6,
        check_vma=False,
    )
```

```python
import itertools

import jax
import jax.numpy as jnp
import numpy as np
from jax import lax
from jax.sharding import PartitionSpec as P

beta_one = 0.9
beta_two = 0.95
bias_one = 1.0 - 0.9**10
bias_two = 1.0 - 0.95**10
rate_value = 0.01
decay_value = 0.1
eps_value = 1e-08


def silu_parts(pre_act):
    sigma = jax.nn.sigmoid(pre_act)
    return (pre_act * sigma, sigma * (1.0 + pre_act * (1.0 - sigma)))


def adam_update(weight, moment, second, gradient):
    moment_new = beta_one * moment + (1.0 - beta_one) * gradient
    second_new = beta_two * second + (1.0 - beta_two) * gradient * gradient
    update = moment_new / bias_one / (jnp.sqrt(second_new / bias_two) + eps_value)
    return (weight - rate_value * (update + decay_value * weight), moment_new, second_new)


def contract_rows(left, right):
    return lax.dot_general(
        left, right, (((0,), (0,)), ((), ())), preferred_element_type=jnp.float32
    )


def slot_permutation(old_owner, new_owner, groups):
    labels = jnp.arange(groups, dtype=jnp.int32)
    dest = jnp.sum(jnp.where(old_owner[:, None] == labels[None, :], new_owner[:, None], 0), axis=0)
    source = jnp.sum(jnp.where(new_owner[:, None] == labels[None, :], old_owner[:, None], 0), axis=0)
    return dest, source


def make_mover(old_owner, new_owner, groups):
    dest, source = slot_permutation(old_owner, new_owner, groups)
    if groups <= 4:
        orders = list(itertools.permutations(range(groups)))
        table = jnp.asarray(np.array(orders, np.int32))
        match = jnp.all(table == dest[None, :], axis=1)
        number = jnp.sum(jnp.where(match, jnp.arange(len(orders), dtype=jnp.int32), 0))

        def branch(order):
            pairs = [(s, d) for s, d in enumerate(order)]
            if all(s == d for s, d in pairs):
                return lambda arrays: arrays
            return lambda arrays: tuple(lax.ppermute(a, "expert", pairs) for a in arrays)

        branches = [branch(order) for order in orders]
        return lambda arrays: lax.switch(number, branches, arrays)

    mine = source[lax.axis_index("expert")]

    def gather_move(arrays):
        return tuple(
            lax.dynamic_index_in_dim(
                lax.all_gather(a, "expert", axis=0, tiled=False), mine, 0, keepdims=False
            )
            for a in arrays
        )

    return gather_move


def local(
    tokens,
    cotangent,
    block_expert,
    block_count,
    old_owner,
    new_owner,
    up_weight,
    down_weight,
    up_first,
    up_second,
    down_first,
    down_second,
):
    groups = lax.axis_size("expert")
    tok_rows, features = tokens.shape
    block_num = block_count.shape[0]
    block_len = tok_rows // block_num
    capacity = 2 * block_num // groups
    move = make_mover(old_owner, new_owner, groups)

    def short(array):
        return array[0].astype(jnp.bfloat16)

    labels = jnp.arange(groups, dtype=jnp.int32)
    block_ids = block_expert[:, 0]
    target = jnp.sum(
        jnp.where(block_ids[:, None] == labels[None, :], new_owner[None, :], 0), axis=1
    )
    earlier = (
        jnp.arange(block_num, dtype=jnp.int32)[:, None]
        > jnp.arange(block_num, dtype=jnp.int32)[None, :]
    )
    same_id = block_ids[:, None] == block_ids[None, :]
    position = jnp.sum(same_id & earlier, axis=1)
    slot_of = target * capacity + position
    placing = (jnp.arange(groups * capacity, dtype=jnp.int32)[:, None] == slot_of[None, :]).astype(
        jnp.bfloat16
    )
    alive = jnp.arange(block_len, dtype=jnp.int32)[None, :] < block_count[:, None]
    zero_value = jnp.zeros((), jnp.bfloat16)

    def dispatch(array):
        blocks = jnp.where(
            alive[:, :, None], array.reshape(block_num, block_len, features), zero_value
        )
        placed = jnp.einsum(
            "sb,btf->stf", placing, blocks, preferred_element_type=jnp.float32
        ).astype(jnp.bfloat16)
        return placed.reshape(groups, capacity * block_len, features)

    def swap(array):
        return lax.all_to_all(array, "expert", split_axis=0, concat_axis=0, tiled=True)

    rows = groups * capacity * block_len

    up_state, down_state = move((short(up_weight), short(down_weight)))
    up_mat = lax.all_gather(up_state, "dp", axis=0, tiled=True)
    down_mat = lax.all_gather(down_state, "dp", axis=0, tiled=True)

    tokens, cotangent, up_state, down_state = lax.optimization_barrier(
        (tokens, cotangent, up_state, down_state)
    )
    inputs = swap(dispatch(tokens)).reshape(rows, features)
    moments = (short(down_first), short(down_second), short(up_first), short(up_second))
    send_dy, moments = lax.optimization_barrier((dispatch(cotangent), moments))
    upstream = swap(send_dy).reshape(rows, features)

    pre_act = jnp.dot(inputs, up_mat, preferred_element_type=jnp.float32)
    active, slopes = silu_parts(pre_act)
    hidden = active.astype(jnp.bfloat16)
    down_part = contract_rows(hidden, upstream).astype(jnp.bfloat16)
    upstream, down_part = lax.optimization_barrier((upstream, down_part))
    down_grad = lax.psum_scatter(down_part, "dp", scatter_dimension=0, tiled=True)
    back_grad = lax.dot_general(
        upstream, down_mat, (((1,), (1,)), ((), ())), preferred_element_type=jnp.float32
    )
    pre_grad = (back_grad * slopes).astype(jnp.bfloat16)
    up_part = contract_rows(inputs, pre_grad).astype(jnp.bfloat16)
    up_grad = lax.psum_scatter(up_part, "dp", scatter_dimension=0, tiled=True)
    input_grad = lax.dot_general(
        pre_grad, up_mat, (((1,), (1,)), ((), ())), preferred_element_type=jnp.float32
    ).astype(jnp.bfloat16)

    moments, _ = lax.optimization_barrier((moments, up_part))
    moments = move(moments)
    input_grad, moments = lax.optimization_barrier((input_grad, moments))
    returned = swap(input_grad.reshape(groups, capacity * block_len, features))
    down_moment, down_square, up_moment, up_square = moments

    def wide(*arrays):
        return tuple(a.astype(jnp.float32) for a in arrays)

    down_new = adam_update(*wide(down_state, down_moment, down_square, down_grad))
    up_moment, down_new = lax.optimization_barrier((up_moment, down_new))
    up_new = adam_update(*wide(up_state, up_moment, up_square, up_grad))
    returned, down_new, up_new = lax.optimization_barrier((returned, down_new, up_new))
    token_grad = jnp.einsum(
        "sb,stf->btf",
        placing,
        returned.reshape(groups * capacity, block_len, features),
        preferred_element_type=jnp.float32,
    )
    token_grad = token_grad.astype(jnp.bfloat16).reshape(tok_rows, features)

    results = (up_new[0], down_new[0], up_new[1], up_new[2], down_new[1], down_new[2])
    return (token_grad,) + tuple(r[None] for r in results)


def solution(mesh):
    state = P("expert", "dp", None)
    row = P(("expert", "dp"), None)
    return jax.shard_map(
        local,
        mesh=mesh,
        in_specs=(row, row, row, P(("expert", "dp")), P(), P()) + (state,) * 6,
        out_specs=(row,) + (state,) * 6,
        check_vma=False,
    )
```

```python
import itertools

import jax
import jax.numpy as jnp
import numpy as np
from jax import lax
from jax.sharding import PartitionSpec as P


beta_one = 0.9
beta_two = 0.95
bias_one = 1.0 - 0.9**10
bias_two = 1.0 - 0.95**10
rate_value = 0.01
decay_value = 0.1
eps_value = 1e-08


def silu_parts(pre_act):
    sigma = jax.nn.sigmoid(pre_act)
    return (pre_act * sigma, sigma * (1.0 + pre_act * (1.0 - sigma)))


def adam_update(weight, moment, second, gradient):
    moment_new = beta_one * moment + (1.0 - beta_one) * gradient
    second_new = beta_two * second + (1.0 - beta_two) * gradient * gradient
    update = moment_new / bias_one / (jnp.sqrt(second_new / bias_two) + eps_value)
    return (weight - rate_value * (update + decay_value * weight), moment_new, second_new)


def contract_rows(left, right):
    return lax.dot_general(
        left, right, (((0,), (0,)), ((), ())), preferred_element_type=jnp.float32
    )


def slot_permutation(old_owner, new_owner, groups):
    labels = jnp.arange(groups, dtype=jnp.int32)
    dest = jnp.sum(jnp.where(old_owner[:, None] == labels[None, :], new_owner[:, None], 0), axis=0)
    source = jnp.sum(jnp.where(new_owner[:, None] == labels[None, :], old_owner[:, None], 0), axis=0)
    return dest, source


def make_mover(old_owner, new_owner, groups):
    dest, source = slot_permutation(old_owner, new_owner, groups)
    if groups <= 4:
        orders = list(itertools.permutations(range(groups)))
        table = jnp.asarray(np.array(orders, np.int32))
        match = jnp.all(table == dest[None, :], axis=1)
        number = jnp.sum(jnp.where(match, jnp.arange(len(orders), dtype=jnp.int32), 0))

        def branch(order):
            pairs = [(s, d) for s, d in enumerate(order)]
            if all(s == d for s, d in pairs):
                return lambda arrays: arrays
            return lambda arrays: tuple(lax.ppermute(a, "expert", pairs) for a in arrays)

        branches = [branch(order) for order in orders]
        return lambda arrays: lax.switch(number, branches, arrays)

    mine = source[lax.axis_index("expert")]

    def gather_move(arrays):
        return tuple(
            lax.dynamic_index_in_dim(
                lax.all_gather(a, "expert", axis=0, tiled=False), mine, 0, keepdims=False
            )
            for a in arrays
        )

    return gather_move


def local(
    tokens,
    cotangent,
    block_expert,
    block_count,
    old_owner,
    new_owner,
    up_weight,
    down_weight,
    up_first,
    up_second,
    down_first,
    down_second,
):
    groups = lax.axis_size("expert")
    tok_rows, features = tokens.shape
    block_num = block_count.shape[0]
    block_len = tok_rows // block_num
    capacity = 2 * block_num // groups
    move = make_mover(old_owner, new_owner, groups)

    def short(array):
        return array[0].astype(jnp.bfloat16)

    labels = jnp.arange(groups, dtype=jnp.int32)
    block_ids = block_expert[:, 0]
    target = jnp.sum(
        jnp.where(block_ids[:, None] == labels[None, :], new_owner[None, :], 0), axis=1
    )
    earlier = (
        jnp.arange(block_num, dtype=jnp.int32)[:, None]
        > jnp.arange(block_num, dtype=jnp.int32)[None, :]
    )
    same_id = block_ids[:, None] == block_ids[None, :]
    position = jnp.sum(same_id & earlier, axis=1)
    slot_of = target * capacity + position
    placing = (jnp.arange(groups * capacity, dtype=jnp.int32)[:, None] == slot_of[None, :]).astype(
        jnp.bfloat16
    )
    alive = jnp.arange(block_len, dtype=jnp.int32)[None, :] < block_count[:, None]
    zero_value = jnp.zeros((), jnp.bfloat16)

    def dispatch(array):
        blocks = jnp.where(
            alive[:, :, None], array.reshape(block_num, block_len, features), zero_value
        )
        placed = jnp.einsum(
            "sb,btf->stf", placing, blocks, preferred_element_type=jnp.float32
        ).astype(jnp.bfloat16)
        return placed.reshape(groups, capacity * block_len, features)

    def swap(array):
        return lax.all_to_all(array, "expert", split_axis=0, concat_axis=0, tiled=True)

    rows = groups * capacity * block_len

    up_state, down_state = move((short(up_weight), short(down_weight)))
    up_mat = lax.all_gather(up_state, "dp", axis=0, tiled=True)
    down_mat = lax.all_gather(down_state, "dp", axis=0, tiled=True)

    tokens, cotangent, up_state, down_state = lax.optimization_barrier(
        (tokens, cotangent, up_state, down_state)
    )
    inputs = swap(dispatch(tokens)).reshape(rows, features)
    moments = (short(down_first), short(down_second), short(up_first), short(up_second))
    send_dy, moments = lax.optimization_barrier((dispatch(cotangent), moments))
    upstream = swap(send_dy).reshape(rows, features)

    pre_act = jnp.dot(inputs, up_mat, preferred_element_type=jnp.float32)
    active, slopes = silu_parts(pre_act)
    hidden = active.astype(jnp.bfloat16)
    down_part = contract_rows(hidden, upstream).astype(jnp.bfloat16)
    upstream, down_part = lax.optimization_barrier((upstream, down_part))
    down_grad = lax.psum_scatter(down_part, "dp", scatter_dimension=0, tiled=True)
    back_grad = lax.dot_general(
        upstream, down_mat, (((1,), (1,)), ((), ())), preferred_element_type=jnp.float32
    )
    pre_grad = (back_grad * slopes).astype(jnp.bfloat16)
    cut = features // 256 * 128

    def rows_grad(grad, mat):
        part = lax.dot_general(
            grad, mat, (((1,), (1,)), ((), ())), preferred_element_type=jnp.float32
        ).astype(jnp.bfloat16)
        return part.reshape(groups, capacity * block_len, mat.shape[0])

    first_half = rows_grad(pre_grad, up_mat[:cut])
    pre_grad, first_half = lax.optimization_barrier((pre_grad, first_half))
    first_half = swap(first_half)
    up_part = contract_rows(inputs, pre_grad).astype(jnp.bfloat16)
    up_grad = lax.psum_scatter(up_part, "dp", scatter_dimension=0, tiled=True)
    second_half = rows_grad(pre_grad, up_mat[cut:])

    moments, _, second_half = lax.optimization_barrier((moments, up_part, second_half))
    moments = move(moments)
    second_half, moments = lax.optimization_barrier((second_half, moments))
    second_half = swap(second_half)
    down_moment, down_square, up_moment, up_square = moments

    def wide(*arrays):
        return tuple(a.astype(jnp.float32) for a in arrays)

    down_new = adam_update(*wide(down_state, down_moment, down_square, down_grad))
    up_moment, down_new = lax.optimization_barrier((up_moment, down_new))
    up_new = adam_update(*wide(up_state, up_moment, up_square, up_grad))
    second_half, down_new, up_new = lax.optimization_barrier((second_half, down_new, up_new))

    def combine(returned):
        back = jnp.einsum(
            "sb,stf->btf",
            placing,
            returned.reshape(groups * capacity, block_len, returned.shape[-1]),
            preferred_element_type=jnp.float32,
        )
        return back.astype(jnp.bfloat16).reshape(tok_rows, returned.shape[-1])

    token_grad = jnp.concatenate((combine(first_half), combine(second_half)), axis=1)
    results = (up_new[0], down_new[0], up_new[1], up_new[2], down_new[1], down_new[2])
    return (token_grad,) + tuple(r[None] for r in results)


def solution(mesh):
    state = P("expert", "dp", None)
    row = P(("expert", "dp"), None)
    return jax.shard_map(
        local,
        mesh=mesh,
        in_specs=(row, row, row, P(("expert", "dp")), P(), P()) + (state,) * 6,
        out_specs=(row,) + (state,) * 6,
        check_vma=False,
    )
```

```python
import itertools

import jax
import jax.numpy as jnp
import numpy as np
from jax import lax
from jax.sharding import PartitionSpec as P

beta_one = 0.9
beta_two = 0.95
bias_one = 1.0 - 0.9**10
bias_two = 1.0 - 0.95**10
rate_value = 0.01
decay_value = 0.1
eps_value = 1e-08


def silu_parts(pre_act):
    sigma = jax.nn.sigmoid(pre_act)
    return (pre_act * sigma, sigma * (1.0 + pre_act * (1.0 - sigma)))


def adam_update(weight, moment, second, gradient):
    moment_new = beta_one * moment + (1.0 - beta_one) * gradient
    second_new = beta_two * second + (1.0 - beta_two) * gradient * gradient
    update = moment_new / bias_one / (jnp.sqrt(second_new / bias_two) + eps_value)
    return (weight - rate_value * (update + decay_value * weight), moment_new, second_new)


def contract_rows(left, right):
    return lax.dot_general(
        left, right, (((0,), (0,)), ((), ())), preferred_element_type=jnp.float32
    )


def slot_permutation(old_owner, new_owner, groups):
    labels = jnp.arange(groups, dtype=jnp.int32)
    dest = jnp.sum(jnp.where(old_owner[:, None] == labels[None, :], new_owner[:, None], 0), axis=0)
    source = jnp.sum(jnp.where(new_owner[:, None] == labels[None, :], old_owner[:, None], 0), axis=0)
    return dest, source


def make_mover(old_owner, new_owner, groups):
    dest, source = slot_permutation(old_owner, new_owner, groups)
    if groups <= 4:
        orders = list(itertools.permutations(range(groups)))
        table = jnp.asarray(np.array(orders, np.int32))
        match = jnp.all(table == dest[None, :], axis=1)
        number = jnp.sum(jnp.where(match, jnp.arange(len(orders), dtype=jnp.int32), 0))

        def branch(order):
            pairs = [(s, d) for s, d in enumerate(order)]
            if all(s == d for s, d in pairs):
                return lambda arrays: arrays
            return lambda arrays: tuple(lax.ppermute(a, "expert", pairs) for a in arrays)

        branches = [branch(order) for order in orders]
        return lambda arrays: lax.switch(number, branches, arrays)

    mine = source[lax.axis_index("expert")]

    def gather_move(arrays):
        return tuple(
            lax.dynamic_index_in_dim(
                lax.all_gather(a, "expert", axis=0, tiled=False), mine, 0, keepdims=False
            )
            for a in arrays
        )

    return gather_move


def local(
    tokens,
    cotangent,
    block_expert,
    block_count,
    old_owner,
    new_owner,
    up_weight,
    down_weight,
    up_first,
    up_second,
    down_first,
    down_second,
):
    groups = lax.axis_size("expert")
    tok_rows, features = tokens.shape
    block_num = block_count.shape[0]
    block_len = tok_rows // block_num
    capacity = 2 * block_num // groups
    move = make_mover(old_owner, new_owner, groups)

    def short(array):
        return array[0].astype(jnp.bfloat16)

    labels = jnp.arange(groups, dtype=jnp.int32)
    block_ids = block_expert[:, 0]
    target = jnp.sum(
        jnp.where(block_ids[:, None] == labels[None, :], new_owner[None, :], 0), axis=1
    )
    earlier = (
        jnp.arange(block_num, dtype=jnp.int32)[:, None]
        > jnp.arange(block_num, dtype=jnp.int32)[None, :]
    )
    same_id = block_ids[:, None] == block_ids[None, :]
    position = jnp.sum(same_id & earlier, axis=1)
    slot_of = target * capacity + position
    placing = (jnp.arange(groups * capacity, dtype=jnp.int32)[:, None] == slot_of[None, :]).astype(
        jnp.bfloat16
    )
    alive = jnp.arange(block_len, dtype=jnp.int32)[None, :] < block_count[:, None]
    zero_value = jnp.zeros((), jnp.bfloat16)

    def dispatch(array):
        blocks = jnp.where(
            alive[:, :, None], array.reshape(block_num, block_len, features), zero_value
        )
        placed = jnp.einsum(
            "sb,btf->stf", placing, blocks, preferred_element_type=jnp.float32
        ).astype(jnp.bfloat16)
        return placed.reshape(groups, capacity * block_len, features)

    def swap(array):
        return lax.all_to_all(array, "expert", split_axis=0, concat_axis=0, tiled=True)

    rows = groups * capacity * block_len

    up_state, down_state = move((short(up_weight), short(down_weight)))
    up_mat = lax.all_gather(up_state, "dp", axis=0, tiled=True)
    down_mat = lax.all_gather(down_state, "dp", axis=0, tiled=True)

    tokens, cotangent, up_state, down_state = lax.optimization_barrier(
        (tokens, cotangent, up_state, down_state)
    )
    inputs = swap(dispatch(tokens)).reshape(rows, features)
    moments = (short(down_first), short(down_second), short(up_first), short(up_second))
    send_dy, moments = lax.optimization_barrier((dispatch(cotangent), moments))
    upstream = swap(send_dy).reshape(rows, features)

    pre_act = jnp.dot(inputs, up_mat, preferred_element_type=jnp.float32)
    active, slopes = silu_parts(pre_act)
    hidden = active.astype(jnp.bfloat16)
    down_part = contract_rows(hidden, upstream).astype(jnp.bfloat16)
    upstream, down_part = lax.optimization_barrier((upstream, down_part))
    down_grad = lax.psum_scatter(down_part, "dp", scatter_dimension=0, tiled=True)
    back_grad = lax.dot_general(
        upstream, down_mat, (((1,), (1,)), ((), ())), preferred_element_type=jnp.float32
    )
    pre_grad = (back_grad * slopes).astype(jnp.bfloat16)
    cut = features // 256 * 128

    def rows_grad(grad, mat):
        part = lax.dot_general(
            grad, mat, (((1,), (1,)), ((), ())), preferred_element_type=jnp.float32
        ).astype(jnp.bfloat16)
        return part.reshape(groups, capacity * block_len, mat.shape[0])

    first_half = rows_grad(pre_grad, up_mat[:cut])
    pre_grad, first_half = lax.optimization_barrier((pre_grad, first_half))
    first_half = swap(first_half)
    up_part = contract_rows(inputs, pre_grad).astype(jnp.bfloat16)
    up_grad = lax.psum_scatter(up_part, "dp", scatter_dimension=0, tiled=True)
    second_half = rows_grad(pre_grad, up_mat[cut:])

    moments, _, second_half = lax.optimization_barrier((moments, up_part, second_half))
    moments = move(moments)
    second_half, moments = lax.optimization_barrier((second_half, moments))
    second_half = swap(second_half)
    down_moment, down_square, up_moment, up_square = moments

    def wide(*arrays):
        return tuple(a.astype(jnp.float32) for a in arrays)

    down_new = adam_update(*wide(down_state, down_moment, down_square, down_grad))
    up_moment, down_new, second_half = lax.optimization_barrier(
        (up_moment, down_new, second_half)
    )
    up_new = adam_update(*wide(up_state, up_moment, up_square, up_grad))

    def combine(returned):
        back = jnp.einsum(
            "sb,stf->btf",
            placing,
            returned.reshape(groups * capacity, block_len, returned.shape[-1]),
            preferred_element_type=jnp.float32,
        )
        return back.astype(jnp.bfloat16).reshape(tok_rows, returned.shape[-1])

    token_grad = jnp.concatenate((combine(first_half), combine(second_half)), axis=1)
    results = (up_new[0], down_new[0], up_new[1], up_new[2], down_new[1], down_new[2])
    return (token_grad,) + tuple(r[None] for r in results)


def solution(mesh):
    state = P("expert", "dp", None)
    row = P(("expert", "dp"), None)
    return jax.shard_map(
        local,
        mesh=mesh,
        in_specs=(row, row, row, P(("expert", "dp")), P(), P()) + (state,) * 6,
        out_specs=(row,) + (state,) * 6,
        check_vma=False,
    )
```
